32 devices in a mesh: rep: 4 (over x, core), fsdp: 8 (over z, y).
Axes of the slice: x: 2, y: 2, z: 4, core: 2. Of those that a mesh axis runs over, the one named last changes fastest.
Arguments:
- layer_input: bfloat16 [24576, 1024], P(('rep', 'fsdp')), may hold values from -6 to 6
- item_ids: int32 [24576], P(('rep', 'fsdp')), may hold values from 0 to 48, as said below
- norm_gain: bfloat16 [1024], P('fsdp'), may hold values from 0.25 to 1.75
- norm_bias: bfloat16 [1024], P('fsdp'), may hold values from -1.5 to 1.5
- joint_weight: bfloat16 [1024, 3072], P('fsdp'), may hold values from -0.1875 to 0.1875
- joint_bias: bfloat16 [2048], P('fsdp'), may hold values from -1.5 to 1.5
- out_weight: bfloat16 [1024, 1024], P('fsdp'), may hold values from -0.5 to 0.5
- out_bias: bfloat16 [1024], P('fsdp'), may hold values from -1.5 to 1.5
- second_gain: bfloat16 [1024], P('fsdp'), may hold values from 0.25 to 1.75
- second_bias: bfloat16 [1024], P('fsdp'), may hold values from -1.5 to 1.5
- up_weight: bfloat16 [1024, 2048], P('fsdp'), may hold values from -0.1875 to 0.1875
- up_bias: bfloat16 [2048], P('fsdp'), may hold values from -1.5 to 1.5
- down_weight: bfloat16 [2048, 1024], P('fsdp'), may hold values from -0.125 to 0.125
- down_bias: bfloat16 [1024], P('fsdp'), may hold values from -1.5 to 1.5
- output_grad: bfloat16 [24576, 1024], P(('rep', 'fsdp')), may hold values from -6 to 6
Outputs:
- layer_output: bfloat16 [24576, 1024], P(('rep', 'fsdp'))
- input_grad: bfloat16 [24576, 1024], P(('rep', 'fsdp'))
- norm_gain_grad: float32 [1024], P('fsdp')
- norm_bias_grad: float32 [1024], P('fsdp')
- joint_weight_grad: float32 [1024, 3072], P('fsdp')
- joint_bias_grad: float32 [2048], P('fsdp')
- out_weight_grad: float32 [1024, 1024], P('fsdp')
- out_bias_grad: float32 [1024], P('fsdp')
- second_gain_grad: float32 [1024], P('fsdp')
- second_bias_grad: float32 [1024], P('fsdp')
- up_weight_grad: float32 [1024, 2048], P('fsdp')
- up_bias_grad: float32 [2048], P('fsdp')
- down_weight_grad: float32 [2048, 1024], P('fsdp')
- down_bias_grad: float32 [1024], P('fsdp')
The draws below stay inside these ranges and needn't reach their ends.
Inputs may be any that keep to these rules, and one draw needn't show every extreme that they name: `item_ids`: every aligned block of 768 rows holds whole items, numbered 0, 1, 2, ... in order of position inside the block; items have 15 or 60 tokens, save at most one item of fewer than 15 tokens in a block, and each block holds at least one item of 60 tokens.
All inputs are finite; a program needn't handle non-finite values.
Results may differ from the reference program's by a relative error of at most 0.018.
Values may be sent and summed in bfloat16 or wider, within the bound.
No kernel may reach another device: no remote copies, remote signals or barrier semaphores. Data moves between devices by JAX's collectives and lax.ppermute only.
A program may use at most 192 MiB of HBM per device.

```python
import jax
import jax.numpy as jnp
from jax import lax

D = 1024
H = 8
HD = 128
FF = 2048
QBLK = 768
TOKENS = 24576


def draw_item_ids(key, part):
    block_count = TOKENS // QBLK
    slot_count = QBLK // 15 + 2
    most_long = max(1, QBLK // 256)
    key_long = jax.random.fold_in(key, 11)
    key_order = jax.random.fold_in(key, 23)
    key_pick = jax.random.fold_in(key, 37)
    long_count = jax.random.randint(key_long, (block_count, 1), 1, most_long + 1)
    chosen_block = jax.random.randint(key_pick, (), 0, block_count)
    block_index = jnp.arange(block_count, dtype=jnp.int32)[:, None]
    long_count = jnp.where(block_index == chosen_block, 1, long_count)
    leftover = QBLK - 60 * long_count
    short_count = leftover // 15
    remainder = leftover - 15 * short_count
    slot_index = jnp.arange(slot_count, dtype=jnp.int32)[None, :]
    item_sizes = jnp.where(slot_index < long_count, 60, jnp.where(slot_index < long_count + short_count, 15, jnp.where(slot_index == long_count + short_count, remainder, 0)))
    random_keys = jax.random.randint(key_order, (block_count, slot_count), 0, 1 << 20) * slot_count + slot_index
    random_keys = jnp.where(item_sizes > 0, random_keys, (1 << 30) + slot_index)
    ranking = jnp.argsort(random_keys, axis=1)
    ordered = jnp.take_along_axis(item_sizes, ranking, axis=1)
    item_ends = jnp.cumsum(ordered, axis=1)
    position = jnp.arange(QBLK, dtype=jnp.int32)
    item_index = jnp.sum((item_ends[:, None, :] <= position[None, :, None]).astype(jnp.int32), axis=2)
    return item_index.reshape(TOKENS).astype(jnp.int32)


def strengthened(drawn, stream_key, source, target, blocks, factor):
    owner, partner = [(jnp.arange(drawn.shape[axis_at]) // (drawn.shape[axis_at] // blocks)).reshape([-1 if axis == axis_at else 1 for axis in range(drawn.ndim)]) for axis_at in (source, target)]
    chosen = jax.random.permutation(stream_key, blocks)[partner]
    strong = (owner == chosen) | (owner == (partner + blocks // 2) % blocks)
    return jnp.where(strong, factor * drawn, drawn)


def block_scale(key, shape, cuts, smallest, largest):
    loudness = 1.0
    for axis_at, parts in cuts:
        steps = jax.random.uniform(jax.random.fold_in(jax.random.fold_in(key, 6), axis_at), (parts,), jnp.float32, smallest / len(cuts), largest / len(cuts))
        loudness = loudness * jnp.repeat(jnp.exp(steps), shape[axis_at] // parts).reshape((-1,) + (1,) * (len(shape) - 1 - axis_at))
    return loudness


def normal_values(rng, dims, scale, most, cuts=(), held_as=jnp.bfloat16):
    array = jax.random.normal(rng, dims, jnp.float32) * scale
    if len(cuts) > 0:
        array = block_scale(rng, dims, cuts, -0.22, 0.18) * array
    return jnp.clip(array, min=-most, max=most).astype(held_as)


def heavy_noise(own_key, extent, scale, most, cuts, heavy, kind=jnp.bfloat16):
    values = scale * jax.random.normal(own_key, extent, jnp.float32)
    if cuts:
        values = values * block_scale(own_key, extent, cuts, -0.22, 0.18)
    return jnp.clip(strengthened(values, jax.random.fold_in(own_key, 3), *heavy), -most, most).astype(kind)


def setup_inputs(seed: int = 0) -> dict:
    seeds = jax.random.split(jax.random.key(seed), 16)
    layer_input = normal_values(seeds[0], (TOKENS, D), 1.0, 6.0, ((0, 32),))
    item_ids = draw_item_ids(jax.random.fold_in(seeds[15], 71), 0)
    norm_gain = jnp.clip(1.0 + 0.15 * jax.random.normal(seeds[2], (D,), jnp.float32), 0.25, 1.75).astype(jnp.bfloat16)
    norm_bias = normal_values(seeds[3], (D,), 0.3, 1.5, ((0, 8),))
    joint_weight = normal_values(seeds[4], (D, 3 * D), D ** -0.5, 0.1875, ((0, 8),))
    joint_bias = normal_values(seeds[5], (2 * D,), 0.3, 1.5, ((0, 8),))
    out_weight = normal_values(seeds[6], (D, D), (D // 8) ** -0.5, 0.5, ((0, 8),))
    out_bias = normal_values(seeds[7], (D,), 0.3, 1.5, ((0, 8),))
    second_gain = jnp.clip(1.0 + 0.15 * jax.random.normal(seeds[8], (D,), jnp.float32), 0.25, 1.75).astype(jnp.bfloat16)
    second_bias = normal_values(seeds[9], (D,), 0.3, 1.5, ((0, 8),))
    up_weight = normal_values(seeds[10], (D, FF), D ** -0.5, 0.1875, ((0, 8),))
    up_bias = normal_values(seeds[11], (FF,), 0.3, 1.5, ((0, 8),))
    down_weight = normal_values(seeds[12], (FF, D), FF ** -0.5, 0.125, ((0, 8),))
    down_bias = normal_values(seeds[13], (D,), 0.3, 1.5, ((0, 8),))
    output_grad = heavy_noise(seeds[14], (TOKENS, D), 1.0, 6.0, ((0, 32),), (0, 1, 32, 2.75))
    return dict(layer_input=layer_input, item_ids=item_ids, norm_gain=norm_gain, norm_bias=norm_bias, joint_weight=joint_weight, joint_bias=joint_bias, out_weight=out_weight, out_bias=out_bias, second_gain=second_gain, second_bias=second_bias, up_weight=up_weight, up_bias=up_bias, down_weight=down_weight, down_bias=down_bias, output_grad=output_grad)


@jax.custom_vjp
def low(v):
    return lax.optimization_barrier(v.astype(jnp.bfloat16)).astype(jnp.float32)

@jax.custom_vjp
def low_back(v):
    return v

def low_keep(v):
    return (low(v), None)

def low_pass(kept, grad):
    return (grad,)

def back_keep(v):
    return (v, None)

def back_low(kept, grad):
    return (low(grad),)
low.defvjp(low_keep, low_pass)
low_back.defvjp(back_keep, back_low)
eps = 1e-05
highest = lax.Precision.HIGHEST

def norm_affine(values, gain, bias):
    center = values - lax.optimization_barrier(jnp.mean(values, axis=-1, keepdims=True))
    spread = lax.optimization_barrier(jnp.mean(center * center, axis=-1, keepdims=True))
    return center * lax.rsqrt(spread + eps) * gain + bias

def attend_block(pieces):
    queries, key_rows, value_rows, labels = pieces
    length = queries.shape[0]
    queries = queries.reshape(length, H, HD)
    key_rows = key_rows.reshape(length, H, HD)
    value_rows = value_rows.reshape(length, H, HD)
    scores = jnp.einsum('qhd,khd->hqk', queries, key_rows, precision=highest) * HD ** (-0.5)
    scores = low_back(scores)
    position = jnp.arange(length)
    allowed = (labels[:, None] == labels[None, :]) & (position[:, None] >= position[None, :])
    scores = jnp.where(allowed[None], scores, -1e+30)
    weights = jax.nn.softmax(scores, axis=-1)
    mixed = jnp.einsum('hqk,khd->qhd', low(weights), value_rows, precision=highest)
    return mixed.reshape(length, H * HD)

def decoder_layer(inputs, labels, params):
    gain_one, bias_one, joint_matrix, joint_shift, out_matrix, out_shift, gain_two, bias_two, up_matrix, up_shift, down_matrix, down_shift = params
    row_count = inputs.shape[0]
    first = low(norm_affine(inputs, gain_one, bias_one))
    projected = jnp.dot(first, joint_matrix, precision=highest)
    offset = jnp.concatenate([joint_shift[:D], jnp.zeros((D,), inputs.dtype), joint_shift[D:]])
    projected = low(low_back(projected + offset))
    blocks = row_count // QBLK
    queries = projected[:, :D].reshape(blocks, QBLK, D)
    key_rows = projected[:, D:2 * D].reshape(blocks, QBLK, D)
    value_rows = projected[:, 2 * D:].reshape(blocks, QBLK, D)
    attended = lax.map(jax.checkpoint(attend_block), (queries, key_rows, value_rows, labels.reshape(blocks, QBLK)))
    attended = low(low_back(attended.reshape(row_count, D)))
    branch = low_back(jnp.dot(attended, out_matrix, precision=highest) + out_shift)
    middle = inputs + branch
    second = low(norm_affine(middle, gain_two, bias_two))
    hidden = low_back(jnp.dot(second, up_matrix, precision=highest) + up_shift)
    active = low(jax.nn.gelu(hidden))
    feed_out = low_back(jnp.dot(active, down_matrix, precision=highest) + down_shift)
    return middle + feed_out

def reference(layer_input, item_ids, norm_gain, norm_bias, joint_weight, joint_bias, out_weight, out_bias, second_gain, second_bias, up_weight, up_bias, down_weight, down_bias, output_grad):
    params = tuple((tensor.astype(jnp.float32) for tensor in (norm_gain, norm_bias, joint_weight, joint_bias, out_weight, out_bias, second_gain, second_bias, up_weight, up_bias, down_weight, down_bias)))
    block_count = TOKENS // QBLK
    per_group = 4 if block_count % 4 == 0 else 1
    groups = block_count // per_group
    group_rows = per_group * QBLK
    inputs = layer_input.reshape(groups, group_rows, D)
    labels = item_ids.reshape(groups, group_rows)
    cotangent = output_grad.reshape(groups, group_rows, D)

    def advance(totals, element):
        rows_in, rows_ids, rows_grad = element

        def runner(values, weights):
            return decoder_layer(values, rows_ids, weights)
        result, puller = jax.vjp(runner, rows_in.astype(jnp.float32), params)
        grad_rows, grad_params = puller(rows_grad.astype(jnp.float32))
        totals = tuple((running + addend for running, addend in zip(totals, grad_params)))
        return (totals, (result.astype(jnp.bfloat16), grad_rows.astype(jnp.bfloat16)))
    initial = tuple((jnp.zeros(weight.shape, jnp.float32) for weight in params))
    totals, (outputs, grads) = lax.scan(advance, initial, (inputs, labels, cotangent))
    return (outputs.reshape(TOKENS, D), grads.reshape(TOKENS, D), totals[0], totals[1], totals[2], totals[3], totals[4], totals[5], totals[6], totals[7], totals[8], totals[9], totals[10], totals[11])
```

```python
import functools

import jax
import jax.numpy as jnp
from jax import lax
from jax.experimental import pallas as pl
from jax.experimental.pallas import tpu as pltpu
from jax.sharding import PartitionSpec as P

H = 8
HD = 128
QBLK = 768
TILE = 128

eps = 1e-05
masked_score = -1e30
AXES = ("rep", "fsdp")


def norm_affine(values, gain, bias):
    center = values - jnp.mean(values, axis=-1, keepdims=True)
    spread = jnp.mean(center * center, axis=-1, keepdims=True)
    return center * lax.rsqrt(spread + eps) * gain + bias


def transposed_dot(left, right, kind=jnp.float32):
    return lax.dot_general(
        left, right, (((0,), (0,)), ((), ())), preferred_element_type=jnp.float32
    ).astype(kind)


def dot_transposed(left, right):
    return lax.dot_general(
        left, right, (((1,), (1,)), ((), ())), preferred_element_type=jnp.float32
    )


def band_weights(q, k, rows_label, cols_label, offset):
    scores = dot_transposed(q, k) * HD ** (-0.5)
    row = lax.broadcasted_iota(jnp.int32, scores.shape, 0)
    col = lax.broadcasted_iota(jnp.int32, scores.shape, 1) + offset
    allowed = (rows_label == cols_label) & (row >= col)
    scores = jnp.where(allowed, scores, masked_score)
    raised = jnp.exp(scores - jnp.max(scores, axis=1, keepdims=True))
    return raised / jnp.sum(raised, axis=1, keepdims=True)


def forward_kernel(q_ref, k_ref, v_ref, rows_ref, cols_ref, out_ref):
    for i in range(QBLK // TILE):
        lo = max(i - 1, 0) * TILE
        hi = (i + 1) * TILE
        own = slice(i * TILE, hi)
        weights = band_weights(
            q_ref[own, :], k_ref[lo:hi, :], rows_ref[own, :], cols_ref[:, lo:hi], lo - i * TILE
        ).astype(jnp.bfloat16)
        out_ref[own, :] = jnp.dot(
            weights, v_ref[lo:hi, :], preferred_element_type=jnp.float32
        ).astype(jnp.bfloat16)


def backward_kernel(q_ref, k_ref, v_ref, up_ref, rows_ref, cols_ref, dq_ref, dk_ref, dv_ref):
    held_k = held_v = None
    for i in range(QBLK // TILE):
        lo = max(i - 1, 0) * TILE
        hi = (i + 1) * TILE
        own = slice(i * TILE, hi)
        q = q_ref[own, :]
        up = up_ref[own, :]
        keys = k_ref[lo:hi, :]
        weights = band_weights(q, keys, rows_ref[own, :], cols_ref[:, lo:hi], lo - i * TILE)
        dweights = dot_transposed(up, v_ref[lo:hi, :])
        inner = jnp.sum(weights * dweights, axis=1, keepdims=True)
        dscores = (weights * (dweights - inner)).astype(jnp.bfloat16)
        dq_ref[own, :] = (
            jnp.dot(dscores, keys, preferred_element_type=jnp.float32) * HD ** (-0.5)
        ).astype(jnp.bfloat16)
        dk = transposed_dot(dscores, q) * HD ** (-0.5)
        dv = transposed_dot(weights.astype(jnp.bfloat16), up)
        if i > 0:
            before = slice(lo, lo + TILE)
            dk_ref[before, :] = (held_k + dk[:TILE]).astype(jnp.bfloat16)
            dv_ref[before, :] = (held_v + dv[:TILE]).astype(jnp.bfloat16)
            dk, dv = dk[TILE:], dv[TILE:]
        held_k, held_v = dk, dv
    last = slice(QBLK - TILE, QBLK)
    dk_ref[last, :] = held_k.astype(jnp.bfloat16)
    dv_ref[last, :] = held_v.astype(jnp.bfloat16)


def head_spec(first_head):
    return pl.BlockSpec((QBLK, HD), lambda b, h: (b, first_head + h))


rows_spec = pl.BlockSpec((QBLK, 1), lambda b, h: (b, 0))
cols_spec = pl.BlockSpec((None, 1, QBLK), lambda b, h: (b, 0, 0))


def attention_forward(projected, rows_label, cols_label):
    rows = projected.shape[0]
    return pl.pallas_call(
        forward_kernel,
        grid=(rows // QBLK, H),
        in_specs=[head_spec(0), head_spec(H), head_spec(2 * H), rows_spec, cols_spec],
        out_specs=head_spec(0),
        out_shape=jax.ShapeDtypeStruct((rows, H * HD), jnp.bfloat16),
        name="attend",
    )(projected, projected, projected, rows_label, cols_label)


def attention_backward(projected, upstream, rows_label, cols_label):
    rows = projected.shape[0]
    shape = jax.ShapeDtypeStruct((rows, H * HD), jnp.bfloat16)
    return pl.pallas_call(
        backward_kernel,
        grid=(rows // QBLK, H),
        in_specs=[head_spec(0), head_spec(H), head_spec(2 * H), head_spec(0), rows_spec, cols_spec],
        out_specs=[head_spec(0)] * 3,
        out_shape=[shape] * 3,
        name="attend_back",
    )(projected, projected, projected, upstream, rows_label, cols_label)


class Plan:
    def __init__(self, reps, shards):
        self.reps, self.shards = reps, shards
        rep_bits = reps.bit_length() - 1
        shard_bits = shards.bit_length() - 1
        assert reps == 1 << rep_bits and shards == 1 << shard_bits and rep_bits > 1 < shard_bits
        f = [("fsdp", b) for b in reversed(range(shard_bits))]
        r = [("rep", b) for b in reversed(range(rep_bits))]
        self.natural = f + r
        self.early = f[:-1] + r[:-2]
        self.side = (r[-2], f[-1])
        self.core = r[-1]

    def swap(self, value, bit):
        axis, place = bit
        pairs = []
        for r in range(self.reps):
            for s in range(self.shards):
                there = (r ^ (1 << place), s) if axis == "rep" else (r, s ^ (1 << place))
                pairs.append((r * self.shards + s, there[0] * self.shards + there[1]))
        return lax.ppermute(value, AXES, pairs)

    @staticmethod
    def mine(bit):
        axis, place = bit
        return (lax.axis_index(axis) >> place) & 1

    def join(self, value, bit):
        other = self.swap(value, bit)
        one = self.mine(bit) == 1
        return jnp.stack([jnp.where(one, other, value), jnp.where(one, value, other)])

    def gather(self, shard):
        rows, cols = shard.shape
        share = rows // self.reps
        held = lax.dynamic_slice_in_dim(shard, lax.axis_index("rep") * share, share, 0)
        done = []
        for bit in self.early:
            held = self.join(held, bit)
            done = [bit] + done
        colors = []
        for color, order in enumerate((self.side, self.side[::-1])):
            part = held[color]
            names = done[1:]
            for bit in (*order, self.core):
                part = self.join(part, bit)
                names = [bit] + names
            wanted = [b for b in self.natural if b != done[0]]
            part = part.transpose([names.index(b) for b in wanted] + [len(names), len(names) + 1])
            colors.append(part)
        return jnp.stack(colors, axis=self.natural.index(done[0]))

    def split(self, value, names, bit):
        at = names.index(bit)
        me = self.mine(bit)
        keep = lax.dynamic_index_in_dim(value, me, at, keepdims=False)
        away = lax.dynamic_index_in_dim(value, 1 - me, at, keepdims=False)
        got = self.swap(away, bit)
        total = (keep.astype(jnp.float32) + got.astype(jnp.float32)).astype(value.dtype)
        return total, names[:at] + names[at + 1 :]

    def reduce(self, value):
        value, names = self.split(value, self.natural, self.core)
        last = self.early[-1]
        at = names.index(last)
        parts = []
        for color, order in enumerate((self.side[::-1], self.side)):
            part = lax.index_in_dim(value, color, at, keepdims=False)
            left = names[:at] + names[at + 1 :]
            for bit in order:
                part, left = self.split(part, left, bit)
            parts.append(part)
        me = self.mine(last) == 1
        keep = jnp.where(me, parts[1], parts[0])
        got = self.swap(jnp.where(me, parts[0], parts[1]), last)
        value = (keep.astype(jnp.float32) + got.astype(jnp.float32)).astype(value.dtype)
        for bit in self.early[:-1][::-1]:
            value, left = self.split(value, left, bit)
        return value

    def spread(self, share):
        for bit in [b for b in self.natural if b[0] == "rep"][::-1]:
            share = self.join(share, bit) if share.ndim == 2 else self.join(share, bit)
        return share.reshape(self.reps, *share.shape[-2:])

    def bits(self, count):
        return (2,) * count

    def parted(self, full):
        rows, cols = full.shape
        n = len(self.natural)
        return full.reshape((2,) * n + (rows >> n, cols))


def packed_vectors(vectors, shards):
    return jnp.concatenate([v.reshape(shards, -1) for v in vectors], axis=1)


def on_device(
    plan,
    layer_input,
    item_ids,
    norm_gain,
    norm_bias,
    joint_weight,
    joint_bias,
    out_weight,
    out_bias,
    second_gain,
    second_bias,
    up_weight,
    up_bias,
    down_weight,
    down_bias,
    output_grad,
):
    rows, width = layer_input.shape
    shards = plan.shards
    blocks = rows // QBLK
    inner = up_weight.shape[1]
    small = (norm_gain, norm_bias, joint_bias, out_bias, second_gain, second_bias, up_bias, down_bias)

    joint_full = plan.gather(joint_weight).reshape(width, 3 * width)
    down_two = down_weight.reshape(plan.reps, 2, -1, width)
    rest = plan.gather(
        jnp.concatenate(
            [
                out_weight,
                up_weight,
                down_two[:, 0].reshape(-1, width),
                down_two[:, 1].reshape(-1, width),
            ],
            axis=1,
        )
    )
    vectors = lax.all_gather(jnp.concatenate(small)[None], "fsdp", axis=0, tiled=True)
    full = []
    at = 0
    for v in small:
        full.append(vectors[:, at : at + v.shape[0]].reshape(-1).astype(jnp.float32))
        at += v.shape[0]
    gain_one, bias_one, shift_joint, shift_out, gain_two, bias_two, shift_up, shift_down = full

    inputs = layer_input.astype(jnp.float32)
    first = norm_affine(inputs, gain_one, bias_one).astype(jnp.bfloat16)
    offset = jnp.concatenate(
        [shift_joint[:width], jnp.zeros((width,), jnp.float32), shift_joint[width:]]
    )
    projected = (
        jnp.dot(first, joint_full, preferred_element_type=jnp.float32) + offset
    ).astype(jnp.bfloat16)
    rows_label = item_ids.reshape(rows, 1)
    cols_label = item_ids.reshape(blocks, 1, QBLK)
    attended = attention_forward(projected, rows_label, cols_label)

    out_full = rest[..., :width].reshape(width, width)
    up_full = rest[..., width : width + inner].reshape(width, inner)
    down_full = jnp.stack(
        [rest[..., width + inner : 2 * width + inner], rest[..., 2 * width + inner :]], axis=-3
    ).reshape(inner, width)

    middle = (
        inputs + jnp.dot(attended, out_full, preferred_element_type=jnp.float32) + shift_out
    )
    second, second_pull = jax.vjp(norm_affine, middle, gain_two, bias_two)
    second = second.astype(jnp.bfloat16)
    hidden = jnp.dot(second, up_full, preferred_element_type=jnp.float32) + shift_up
    active, gelu_pull = jax.vjp(jax.nn.gelu, hidden)
    active = active.astype(jnp.bfloat16)

    upstream = output_grad.astype(jnp.float32)
    grad_down = transposed_dot(active, output_grad, jnp.bfloat16)
    own_down = plan.reduce(plan.parted(grad_down))
    grad_down_shift = jnp.sum(upstream, axis=0)
    dhidden = gelu_pull(dot_transposed(output_grad, down_full))[0].astype(jnp.bfloat16)
    grad_up = transposed_dot(second, dhidden, jnp.bfloat16)
    own_up = plan.reduce(plan.parted(grad_up))
    grad_up_shift = jnp.sum(dhidden.astype(jnp.float32), axis=0)
    dsecond = dot_transposed(dhidden, up_full)
    dmiddle_part, grad_gain_two, grad_bias_two = second_pull(dsecond)
    dmiddle = upstream + dmiddle_part

    dbranch = dmiddle.astype(jnp.bfloat16)
    grad_out = transposed_dot(attended, dbranch, jnp.bfloat16)
    own_out = plan.reduce(plan.parted(grad_out))
    grad_out_shift = jnp.sum(dbranch.astype(jnp.float32), axis=0)
    dattended = dot_transposed(dbranch, out_full).astype(jnp.bfloat16)
    dprojected = jnp.concatenate(
        attention_backward(projected, dattended, rows_label, cols_label), axis=1
    )
    grad_joint = transposed_dot(first, dprojected, jnp.bfloat16)
    sums = jnp.sum(dprojected.astype(jnp.float32), axis=0)
    grad_joint_shift = jnp.concatenate([sums[:width], sums[2 * width :]])
    dfirst = dot_transposed(dprojected, joint_full)
    first_again, first_pull = jax.vjp(norm_affine, inputs, gain_one, bias_one)
    dinput_part, grad_gain_one, grad_bias_one = first_pull(dfirst)
    input_grad = (dmiddle + dinput_part).astype(jnp.bfloat16)

    layer_output = (
        middle + jnp.dot(active, down_full, preferred_element_type=jnp.float32) + shift_down
    ).astype(jnp.bfloat16)

    small_grads = (
        grad_gain_one,
        grad_bias_one,
        grad_joint_shift,
        grad_out_shift,
        grad_gain_two,
        grad_bias_two,
        grad_up_shift,
        grad_down_shift,
    )
    joint_parts = plan.parted(grad_joint)
    share = joint_parts.shape[-2]
    packed = packed_vectors(small_grads, shards).astype(jnp.bfloat16)
    count = packed.shape[1]
    room = plan.reps * share * HD
    packed = jnp.pad(packed, ((0, 0), (0, room - count)))
    joint_parts = jnp.concatenate(
        [joint_parts, packed.reshape(joint_parts.shape[:-1] + (HD,))], axis=-1
    )
    own_joint = plan.reduce(joint_parts)

    half = own_down.shape[0] // 2
    own_rest = plan.spread(
        jnp.concatenate([own_out, own_up, own_down[:half], own_down[half:]], axis=1)
    ).astype(jnp.float32)
    joint_all = plan.spread(own_joint).astype(jnp.float32)

    out_rows = own_rest[..., :width].reshape(-1, width)
    up_rows = own_rest[..., width : width + inner].reshape(-1, inner)
    down_rows = jnp.stack(
        [own_rest[..., width + inner : 2 * width + inner], own_rest[..., 2 * width + inner :]],
        axis=1,
    ).reshape(-1, width)
    joint_rows = joint_all[..., : 3 * width].reshape(-1, 3 * width)
    flat = joint_all[..., 3 * width :].reshape(-1)
    pieces = []
    at = 0
    for v in small:
        pieces.append(flat[at : at + v.shape[0]])
        at += v.shape[0]
    return (
        layer_output,
        input_grad,
        pieces[0],
        pieces[1],
        joint_rows,
        pieces[2],
        out_rows,
        pieces[3],
        pieces[4],
        pieces[5],
        up_rows,
        pieces[6],
        down_rows,
        pieces[7],
    )


def solution(mesh):
    vector, matrix = P("fsdp"), P("fsdp", None)
    tokens = P(("rep", "fsdp"), None)
    params = (vector, vector, matrix, vector, matrix, vector, vector, vector, matrix, vector, matrix, vector)
    plan = Plan(mesh.shape["rep"], mesh.shape["fsdp"])
    return jax.shard_map(
        functools.partial(on_device, plan),
        mesh=mesh,
        in_specs=(tokens, P(("rep", "fsdp")), *params, tokens),
        out_specs=(tokens, tokens, *params),
        check_vma=False,
    )
```
